32 devices in a mesh: row: 4 (over z), col: 8 (over y, x, core).
Axes of the slice: x: 2, y: 2, z: 4, core: 2. Of those that a mesh axis runs over, the one named last changes fastest.
Arguments:
- tokens: bfloat16 [512, 8192], P('col', 'row'), may hold values from -6 to 6
- w_gate: bfloat16 [8192, 16384], P('row', 'col'), may hold values from -0.09375 to 0.09375
- w_up: bfloat16 [8192, 16384], P('row', 'col'), may hold values from -0.09375 to 0.09375
- w_down: bfloat16 [16384, 8192], P('col', 'row'), may hold values from -0.0625 to 0.0625
- mask_in: int32 [64, 32], P('col', 'row'), may hold values 0 or 1
- mask_out: int32 [64, 32], P('col', 'row'), may hold values 0 or 1
- out_grad: bfloat16 [512, 8192], P('col', 'row'), may hold values from -6 to 6
Outputs:
- output: bfloat16 [512, 8192], P('col', 'row')
- tokens_grad: bfloat16 [512, 8192], P('col', 'row')
- gate_wgrad: bfloat16 [8192, 16384], P('row', 'col')
- up_wgrad: bfloat16 [8192, 16384], P('row', 'col')
- down_wgrad: bfloat16 [16384, 8192], P('col', 'row')
The draws below stay inside these ranges and needn't reach their ends.
All inputs are finite; a program needn't handle non-finite values. No bound on the sum of `mask_in` or of `mask_out` on one device may be relied on, other than what follows from the above.
Results may differ from the reference program's by a relative error of at most 0.0049.
Values may be sent and summed in bfloat16 or wider, within the bound.
A program may use at most 128 MiB of HBM per device.

```python
import jax
import jax.numpy as jnp

D = 8192
FF = 16384
BLOCK = 256
TOKENS = 512
FFB = 64
DB = 32


def touch_ends(values, stream_key, smallest, top_value):
    longest = values.shape.index(max(values.shape))
    spots = []
    for shift in (0, 1):
        where = [jax.random.randint(jax.random.fold_in(stream_key, axis), (), 0, length) for axis, length in enumerate(values.shape)]
        where[longest] = (where[longest] + shift) % values.shape[longest]
        spots.append(tuple(where))
    return values.at[spots[0]].set(smallest).at[spots[1]].set(top_value)


def level_of(stream_key, shape, split, smallest, high):
    gain, own = 1.0, jax.random.fold_in(stream_key, 6)
    for axis_at, parts in split:
        draws = jnp.exp(jax.random.uniform(jax.random.fold_in(own, axis_at), (parts,), jnp.float32, smallest / len(split), high / len(split)))
        gain = gain * jnp.repeat(draws, shape[axis_at] // parts).reshape([-1 if axis == axis_at else 1 for axis in range(len(shape))])
    return gain


def centred(rng, shape, scale, most, split=(), held_as=jnp.bfloat16):
    entries = scale * jax.random.normal(rng, shape, jnp.float32)
    if split:
        entries = entries * level_of(rng, shape, split, -0.22, 0.18)
    return jnp.clip(entries, -most, most).astype(held_as)


def setup_inputs(seed: int = 0) -> dict:
    streams_of = jax.random.split(jax.random.key(seed), 8)
    return {
        "tokens": centred(streams_of[0], (TOKENS, D), 1.0, 6.0, ((0, 8), (1, 4))),
        "w_gate": centred(streams_of[1], (D, FF), (D // 2) ** -0.5, 0.09375, ((0, 4), (1, 8))),
        "w_up": centred(streams_of[2], (D, FF), (D // 2) ** -0.5, 0.09375, ((0, 4), (1, 8))),
        "w_down": centred(streams_of[3], (FF, D), (FF // 2) ** -0.5, 0.0625, ((0, 8), (1, 4))),
        "mask_in": touch_ends((jax.random.randint(streams_of[4], (FFB, DB), 0, 2) < 1).astype(jnp.int32), jax.random.fold_in(streams_of[4], 1), 0, 1),
        "mask_out": touch_ends((jax.random.randint(streams_of[5], (FFB, DB), 0, 2) < 1).astype(jnp.int32), jax.random.fold_in(streams_of[5], 1), 0, 1),
        "out_grad": centred(streams_of[6], (TOKENS, D), 1.0, 6.0, ((0, 8), (1, 4))),
    }


def spread(mask_tile):
    return jnp.repeat(jnp.repeat(mask_tile.T, BLOCK, axis=0), BLOCK, axis=1)


def reference(tokens, w_gate, w_up, w_down, mask_in, mask_out, out_grad):
    keep_in = spread(mask_in).astype(jnp.bfloat16)
    keep_out = spread(mask_out).T.astype(jnp.bfloat16)
    gate_masked = w_gate * keep_in
    up_masked = w_up * keep_in
    down_masked = w_down * keep_out
    gate = jnp.dot(tokens, gate_masked, preferred_element_type=jnp.float32)
    up = jnp.dot(tokens, up_masked, preferred_element_type=jnp.float32)
    sigmoid_gate = jax.nn.sigmoid(gate)
    hidden = (gate * sigmoid_gate * up).astype(jnp.bfloat16)
    output = jnp.dot(hidden, down_masked, preferred_element_type=jnp.float32).astype(jnp.bfloat16)
    hidden_grad = jnp.dot(out_grad, down_masked.T, preferred_element_type=jnp.float32)
    up_grad = (hidden_grad * gate * sigmoid_gate).astype(jnp.bfloat16)
    gate_grad = (hidden_grad * up * sigmoid_gate * (1.0 + gate * (1.0 - sigmoid_gate))).astype(jnp.bfloat16)
    down_wgrad = (jnp.dot(hidden.T, out_grad, preferred_element_type=jnp.float32) * keep_out.astype(jnp.float32)).astype(jnp.bfloat16)
    gate_wgrad = (jnp.dot(tokens.T, gate_grad, preferred_element_type=jnp.float32) * keep_in.astype(jnp.float32)).astype(jnp.bfloat16)
    up_wgrad = (jnp.dot(tokens.T, up_grad, preferred_element_type=jnp.float32) * keep_in.astype(jnp.float32)).astype(jnp.bfloat16)
    tokens_grad = (jnp.dot(gate_grad, gate_masked.T, preferred_element_type=jnp.float32)
                   + jnp.dot(up_grad, up_masked.T, preferred_element_type=jnp.float32)).astype(jnp.bfloat16)
    return (output, tokens_grad, gate_wgrad, up_wgrad, down_wgrad)
```

```python
import functools

import jax
import jax.numpy as jnp
from jax import lax
from jax.experimental import pallas as pl
from jax.experimental.pallas import tpu as pltpu
from jax.sharding import PartitionSpec as P

BLOCK = 256
HALVES = 2
SLOTS = 4
LAG = 2
MESH = pl.DeviceIdType.MESH
F32 = jnp.float32
BF16 = jnp.bfloat16


def dot(left, right, dims):
    return lax.dot_general(left, right, (dims, ((), ())), preferred_element_type=F32)


def step_kernel(
    rows, cols, units,
    tok, cot, w_gate, w_up, w_down, keep_in, keep_out,
    out, tok_grad, x_out, dy_out, fin_out,
    x, dy, part, other, fin, own, w_in, w_dn, out_acc, tok_acc, rs_send, rs_recv,
    ag_ss, ag_rs, loc_s, w_s, p_ss, a_rs, b_rs, fi_ss, fo_ss, f_rs, x_s, fin_s, rs_ss, rs_rs,
):
    r = lax.axis_index("row")
    c = lax.axis_index("col")
    low = r < rows // 2
    inner = jnp.where(low, r + 1, r - 1)
    outer = jnp.where(low, r - 1, r + 1)
    has_outer = (r > 0) & (r < rows - 1)
    middle = (r == rows // 2 - 1) | (r == rows // 2)
    my_turn = jnp.where(low, 0, 1)
    share = tok.shape[0]
    width = x.shape[1]
    half = x.shape[0] // HALVES
    pieces = width // BLOCK

    def owns(k):
        return middle & (k % 2 == my_turn)

    def weights(k):
        s = k % SLOTS
        at = pl.ds(pl.multiple_of(k * BLOCK, BLOCK), BLOCK)
        return (
            pltpu.make_async_copy(w_gate.at[:, at], w_in.at[s, 0], w_s.at[s, 0]),
            pltpu.make_async_copy(w_up.at[:, at], w_in.at[s, 1], w_s.at[s, 1]),
            pltpu.make_async_copy(w_down.at[at, :], w_dn.at[s], w_s.at[s, 2]),
        )

    for copy in weights(0):
        copy.start()

    barrier = pltpu.get_barrier_semaphore()
    pl.semaphore_signal(barrier, inc=1, device_id=(inner, c), device_id_type=MESH)

    @pl.when(has_outer)
    def _():
        pl.semaphore_signal(barrier, inc=1, device_id=(outer, c), device_id_type=MESH)

    for i in range(1, cols):
        pl.semaphore_signal(
            barrier, inc=1, device_id=(r, lax.rem(c + i, cols)), device_id_type=MESH
        )
    pl.semaphore_wait(barrier, jnp.where(has_outer, cols + 1, cols))

    mine = pl.ds(pl.multiple_of(c * share, share), share)

    def gathers(j):
        src, dst = ((tok, x), (cot, dy))[j]
        return [
            pltpu.make_async_remote_copy(
                src_ref=src,
                dst_ref=dst.at[mine, :],
                send_sem=ag_ss.at[j, i - 1],
                recv_sem=ag_rs.at[j, i - 1],
                device_id=(r, lax.rem(c + i, cols)),
                device_id_type=MESH,
            )
            for i in range(1, cols)
        ]

    def own_copy(j):
        src, dst = ((tok, x), (cot, dy))[j]
        return pltpu.make_async_copy(src, dst.at[mine, :], loc_s.at[j])

    def saved(j):
        return pltpu.make_async_copy((x, dy)[j], (x_out, dy_out)[j], x_s.at[j])

    def gathered(j):
        own_copy(j).wait()
        for copy in gathers(j):
            copy.wait()
        saved(j).start()

    for j in range(2):
        own_copy(j).start()
        for copy in gathers(j):
            copy.start()

    out_acc[...] = jnp.zeros_like(out_acc)
    tok_acc[...] = jnp.zeros_like(tok_acc)
    gathered(0)

    def send_inner(k, h):
        return pltpu.make_async_remote_copy(
            src_ref=part.at[k, h], dst_ref=part.at[k, h], send_sem=p_ss.at[k, h],
            recv_sem=a_rs.at[k, h], device_id=(inner, c), device_id_type=MESH,
        )

    def send_middle(k, h):
        return pltpu.make_async_remote_copy(
            src_ref=part.at[k, h], dst_ref=other.at[k // 2, h], send_sem=p_ss.at[k, h],
            recv_sem=b_rs.at[k // 2, h], device_id=(inner, c), device_id_type=MESH,
        )

    def share_inner(k, h):
        return pltpu.make_async_remote_copy(
            src_ref=fin.at[k, h], dst_ref=fin.at[k, h], send_sem=fi_ss.at[k, h],
            recv_sem=f_rs.at[k, h], device_id=(inner, c), device_id_type=MESH,
        )

    def share_outer(k, h):
        return pltpu.make_async_remote_copy(
            src_ref=fin.at[k, h], dst_ref=fin.at[k, h], send_sem=fo_ss.at[k, h],
            recv_sem=f_rs.at[k, h], device_id=(outer, c), device_id_type=MESH,
        )

    def save_fin(k, h):
        return pltpu.make_async_copy(
            fin.at[k, h],
            fin_out.at[
                :,
                pl.ds(pl.multiple_of(h * half, half), half),
                pl.ds(pl.multiple_of(k * BLOCK, BLOCK), BLOCK),
            ],
            fin_s.at[k, h],
        )

    def produce(k):
        s = k % SLOTS
        for copy in weights(k):
            copy.wait()

        @pl.when(k + 1 < units)
        def _():
            for copy in weights(k + 1):
                copy.start()

        @pl.loop(0, pieces)
        def _(i):
            at = pl.ds(pl.multiple_of(i * BLOCK, BLOCK), BLOCK)
            keep = keep_in[k, i]
            w_in[s, 0, at, :] = (w_in[s, 0, at, :].astype(F32) * keep).astype(BF16)
            w_in[s, 1, at, :] = (w_in[s, 1, at, :].astype(F32) * keep).astype(BF16)
            w_dn[s, :, at] = (w_dn[s, :, at].astype(F32) * keep_out[k, i]).astype(BF16)

        @pl.loop(0, HALVES)
        def _(h):
            at = pl.ds(pl.multiple_of(h * half, half), half)
            own[k % 2, h, 0] = dot(x[at, :], w_in[s, 0], ((1,), (0,)))
            own[k % 2, h, 1] = dot(x[at, :], w_in[s, 1], ((1,), (0,)))

        @pl.when(k == 0)
        def _():
            gathered(1)

        @pl.loop(0, HALVES)
        def _(h):
            at = pl.ds(pl.multiple_of(h * half, half), half)
            own[k % 2, h, 2] = dot(dy[at, :], w_dn[s], ((1,), (1,)))

    def combine(k):
        b = k % 2

        @pl.loop(0, HALVES)
        def _(h):
            @pl.when(has_outer)
            def _():
                send_inner(k, h).wait_recv()
                for j in range(3):
                    own[b, h, j] += part[k, h, j].astype(F32)

            @pl.when(owns(k))
            def _():
                send_middle(k, h).wait_recv()
                gate = own[b, h, 0] + other[k // 2, h, 0].astype(F32)
                up = own[b, h, 1] + other[k // 2, h, 1].astype(F32)
                grad = own[b, h, 2] + other[k // 2, h, 2].astype(F32)
                sig = jax.nn.sigmoid(gate)
                act = gate * sig
                fin[k, h, 0] = (act * up).astype(BF16)
                fin[k, h, 1] = (grad * up * sig * (1.0 + gate * (1.0 - sig))).astype(BF16)
                fin[k, h, 2] = (grad * act).astype(BF16)
                share_inner(k, h).start()

            @pl.when(jnp.logical_not(owns(k)))
            def _():
                for j in range(3):
                    part[k, h, j] = own[b, h, j].astype(BF16)

                @pl.when(middle)
                def _():
                    send_middle(k, h).start()

                @pl.when(jnp.logical_not(middle))
                def _():
                    send_inner(k, h).start()

            @pl.when(owns(k) & has_outer)
            def _():
                share_outer(k, h).start()

    def consume(k):
        s = k % SLOTS

        @pl.loop(0, HALVES)
        def _(h):
            @pl.when(jnp.logical_not(owns(k)))
            def _():
                share_inner(k, h).wait_recv()

                @pl.when(has_outer)
                def _():
                    share_outer(k, h).start()

            save_fin(k, h).start()

        @pl.loop(0, HALVES)
        def _(h):
            at = pl.ds(pl.multiple_of(h * half, half), half)
            out_acc[at, :] += dot(fin[k, h, 0], w_dn[s], ((1,), (0,)))
            tok_acc[at, :] += dot(fin[k, h, 1], w_in[s, 0], ((1,), (1,))) + dot(
                fin[k, h, 2], w_in[s, 1], ((1,), (1,))
            )

    @pl.loop(0, units + LAG)
    def _(t):
        @pl.when(t < units)
        def _():
            produce(t)

        @pl.when((t >= 1) & (t <= units))
        def _():
            combine(t - 1)

        @pl.when(t >= LAG)
        def _():
            consume(t - LAG)

    def scatters(j):
        return [
            pltpu.make_async_remote_copy(
                src_ref=rs_send.at[
                    j, pl.ds(pl.multiple_of(lax.rem(c + i, cols) * share, share), share), :
                ],
                dst_ref=rs_recv.at[j, i - 1],
                send_sem=rs_ss.at[j, i - 1],
                recv_sem=rs_rs.at[j, i - 1],
                device_id=(r, lax.rem(c + i, cols)),
                device_id_type=MESH,
            )
            for i in range(1, cols)
        ]

    for j, acc in enumerate((out_acc, tok_acc)):
        rs_send[j] = acc[...].astype(BF16)
        for copy in scatters(j):
            copy.start()

    @pl.loop(0, units * HALVES)
    def _(n):
        k, h = n // HALVES, n % HALVES
        save_fin(k, h).wait()

        @pl.when(owns(k))
        def _():
            share_inner(k, h).wait_send()

        @pl.when(jnp.logical_not(owns(k)))
        def _():
            send_inner(k, h).wait_send()

        @pl.when(has_outer)
        def _():
            share_outer(k, h).wait_send()

    for j in range(2):
        saved(j).wait()

    for j, (acc, ref) in enumerate(((out_acc, out), (tok_acc, tok_grad))):
        for copy in scatters(j):
            copy.wait()
        total = acc[mine, :]
        for i in range(cols - 1):
            total = total + rs_recv[j, i].astype(F32)
        ref[...] = total.astype(BF16)


def wgrad_kernel(x, dy, fin, keep_in, keep_out, gate_w, up_w, down_w, x_t, h_t):
    k = pl.program_id(0)
    pieces = x.shape[1] // BLOCK

    @pl.when(k == 0)
    def _():
        @pl.loop(0, pieces)
        def _(i):
            at = pl.ds(pl.multiple_of(i * BLOCK, BLOCK), BLOCK)
            x_t[at, :] = x[:, at].T

    h_t[...] = fin[0].T

    @pl.loop(0, pieces)
    def _(i):
        at = pl.ds(pl.multiple_of(i * BLOCK, BLOCK), BLOCK)

        @pl.when(keep_in[k, i] != 0)
        def _():
            gate_w[at, :] = dot(x_t[at, :], fin[1], ((1,), (0,))).astype(BF16)
            up_w[at, :] = dot(x_t[at, :], fin[2], ((1,), (0,))).astype(BF16)

        @pl.when(keep_in[k, i] == 0)
        def _():
            gate_w[at, :] = jnp.zeros((BLOCK, BLOCK), BF16)
            up_w[at, :] = jnp.zeros((BLOCK, BLOCK), BF16)

        @pl.when(keep_out[k, i] != 0)
        def _():
            down_w[:, at] = dot(h_t[...], dy[:, at], ((1,), (0,))).astype(BF16)

        @pl.when(keep_out[k, i] == 0)
        def _():
            down_w[:, at] = jnp.zeros((BLOCK, BLOCK), BF16)


def local(rows, cols, tokens, w_gate, w_up, w_down, mask_in, mask_out, out_grad):
    share, width = tokens.shape
    hidden = w_gate.shape[1]
    units = hidden // BLOCK
    total = share * cols
    half = total // HALVES
    vmem = pl.BlockSpec(memory_space=pltpu.VMEM)
    smem = pl.BlockSpec(memory_space=pltpu.SMEM)
    anywhere = pl.BlockSpec(memory_space=pl.ANY)
    dma = pltpu.SemaphoreType.DMA
    sent = (units, HALVES)
    flops = 12 * total * width * hidden
    output, tokens_grad, x, dy, fin = pl.pallas_call(
        functools.partial(step_kernel, rows, cols, units),
        out_shape=(
            jax.ShapeDtypeStruct((share, width), BF16),
            jax.ShapeDtypeStruct((share, width), BF16),
            jax.ShapeDtypeStruct((total, width), BF16),
            jax.ShapeDtypeStruct((total, width), BF16),
            jax.ShapeDtypeStruct((3, total, hidden), BF16),
        ),
        in_specs=[vmem, vmem, anywhere, anywhere, anywhere, smem, smem],
        out_specs=(vmem, vmem, anywhere, anywhere, anywhere),
        scratch_shapes=[
            pltpu.VMEM((total, width), BF16),
            pltpu.VMEM((total, width), BF16),
            pltpu.VMEM((units, HALVES, 3, half, BLOCK), BF16),
            pltpu.VMEM(((units + 1) // 2, HALVES, 3, half, BLOCK), BF16),
            pltpu.VMEM((units, HALVES, 3, half, BLOCK), BF16),
            pltpu.VMEM((2, HALVES, 3, half, BLOCK), F32),
            pltpu.VMEM((SLOTS, 2, width, BLOCK), BF16),
            pltpu.VMEM((SLOTS, BLOCK, width), BF16),
            pltpu.VMEM((total, width), F32),
            pltpu.VMEM((total, width), F32),
            pltpu.VMEM((2, total, width), BF16),
            pltpu.VMEM((2, cols - 1, share, width), BF16),
            dma((2, cols - 1)),
            dma((2, cols - 1)),
            dma((2,)),
            dma((SLOTS, 3)),
            dma(sent),
            dma(sent),
            dma(((units + 1) // 2, HALVES)),
            dma(sent),
            dma(sent),
            dma(sent),
            dma((2,)),
            dma(sent),
            dma((2, cols - 1)),
            dma((2, cols - 1)),
        ],
        compiler_params=pltpu.CompilerParams(
            collective_id=0, has_side_effects=True, vmem_limit_bytes=63 * 1024 * 1024
        ),
        cost_estimate=pl.CostEstimate(
            flops=flops, bytes_accessed=6 * width * hidden, transcendentals=total * hidden
        ),
        name="step",
    )(
        tokens, out_grad, w_gate, w_up, w_down,
        mask_in.astype(F32), mask_out.astype(F32),
    )
    gate_wgrad, up_wgrad, down_wgrad = pl.pallas_call(
        wgrad_kernel,
        grid=(units,),
        out_shape=(
            jax.ShapeDtypeStruct((width, hidden), BF16),
            jax.ShapeDtypeStruct((width, hidden), BF16),
            jax.ShapeDtypeStruct((hidden, width), BF16),
        ),
        in_specs=[
            pl.BlockSpec((total, width), lambda k: (0, 0)),
            pl.BlockSpec((total, width), lambda k: (0, 0)),
            pl.BlockSpec((3, total, BLOCK), lambda k: (0, 0, k)),
            smem,
            smem,
        ],
        out_specs=(
            pl.BlockSpec((width, BLOCK), lambda k: (0, k)),
            pl.BlockSpec((width, BLOCK), lambda k: (0, k)),
            pl.BlockSpec((BLOCK, width), lambda k: (k, 0)),
        ),
        scratch_shapes=[pltpu.VMEM((width, total), BF16), pltpu.VMEM((BLOCK, total), BF16)],
        compiler_params=pltpu.CompilerParams(vmem_limit_bytes=40 * 1024 * 1024),
        name="wgrad",
    )(x, dy, fin, mask_in, mask_out)
    return output, tokens_grad, gate_wgrad, up_wgrad, down_wgrad


def solution(mesh):
    placed = (
        P("col", "row"),
        P("row", "col"),
        P("row", "col"),
        P("col", "row"),
        P("col", "row"),
        P("col", "row"),
        P("col", "row"),
    )
    return jax.shard_map(
        functools.partial(local, mesh.shape["row"], mesh.shape["col"]),
        mesh=mesh,
        in_specs=placed,
        out_specs=(
            P("col", "row"),
            P("col", "row"),
            P("row", "col"),
            P("row", "col"),
            P("col", "row"),
        ),
        check_vma=False,
    )
```

```python
import functools

import jax
import jax.numpy as jnp
from jax import lax
from jax.experimental import pallas as pl
from jax.experimental.pallas import tpu as pltpu
from jax.sharding import PartitionSpec as P

BLOCK = 256
HALVES = 2
SLOTS = 7
LAG = 5
MESH = pl.DeviceIdType.MESH
F32 = jnp.float32
BF16 = jnp.bfloat16


def dot(left, right, dims):
    return lax.dot_general(left, right, (dims, ((), ())), preferred_element_type=F32)


def step_kernel(
    rows, cols, units,
    tok, cot, w_gate, w_up, w_down, keep_in, keep_out,
    out, tok_grad, x_out, dy_out, fin_out,
    x, dy, part, other, fin, own, w_in, w_dn, out_acc, tok_acc, rs_send, rs_recv,
    ag_ss, ag_rs, loc_s, w_s, p_ss, a_rs, b_rs, fi_ss, fo_ss, f_rs, x_s, fin_s, rs_ss, rs_rs,
):
    r = lax.axis_index("row")
    c = lax.axis_index("col")
    low = r < rows // 2
    inner = jnp.where(low, r + 1, r - 1)
    outer = jnp.where(low, r - 1, r + 1)
    has_outer = (r > 0) & (r < rows - 1)
    middle = (r == rows // 2 - 1) | (r == rows // 2)
    my_turn = jnp.where(low, 0, 1)
    share = tok.shape[0]
    width = x.shape[1]
    half = x.shape[0] // HALVES
    pieces = width // BLOCK

    def owns(k):
        return middle & (k % 2 == my_turn)

    def weights(k):
        s = k % SLOTS
        at = pl.ds(pl.multiple_of(k * BLOCK, BLOCK), BLOCK)
        return (
            pltpu.make_async_copy(w_gate.at[:, at], w_in.at[s, 0], w_s.at[s, 0]),
            pltpu.make_async_copy(w_up.at[:, at], w_in.at[s, 1], w_s.at[s, 1]),
            pltpu.make_async_copy(w_down.at[at, :], w_dn.at[s], w_s.at[s, 2]),
        )

    for copy in weights(0):
        copy.start()

    barrier = pltpu.get_barrier_semaphore()
    pl.semaphore_signal(barrier, inc=1, device_id=(inner, c), device_id_type=MESH)

    @pl.when(has_outer)
    def _():
        pl.semaphore_signal(barrier, inc=1, device_id=(outer, c), device_id_type=MESH)

    for i in range(1, cols):
        pl.semaphore_signal(
            barrier, inc=1, device_id=(r, lax.rem(c + i, cols)), device_id_type=MESH
        )
    pl.semaphore_wait(barrier, jnp.where(has_outer, cols + 1, cols))

    mine = pl.ds(pl.multiple_of(c * share, share), share)

    def gathers(j):
        src, dst = ((tok, x), (cot, dy))[j]
        return [
            pltpu.make_async_remote_copy(
                src_ref=src,
                dst_ref=dst.at[mine, :],
                send_sem=ag_ss.at[j, i - 1],
                recv_sem=ag_rs.at[j, i - 1],
                device_id=(r, lax.rem(c + i, cols)),
                device_id_type=MESH,
            )
            for i in range(1, cols)
        ]

    def own_copy(j):
        src, dst = ((tok, x), (cot, dy))[j]
        return pltpu.make_async_copy(src, dst.at[mine, :], loc_s.at[j])

    def saved(j):
        return pltpu.make_async_copy((x, dy)[j], (x_out, dy_out)[j], x_s.at[j])

    def gathered(j):
        own_copy(j).wait()
        for copy in gathers(j):
            copy.wait()
        saved(j).start()

    for j in range(2):
        own_copy(j).start()
        for copy in gathers(j):
            copy.start()

    out_acc[...] = jnp.zeros_like(out_acc)
    tok_acc[...] = jnp.zeros_like(tok_acc)
    gathered(0)

    def send_inner(k, h):
        return pltpu.make_async_remote_copy(
            src_ref=part.at[k, h], dst_ref=part.at[k, h], send_sem=p_ss.at[k, h],
            recv_sem=a_rs.at[k, h], device_id=(inner, c), device_id_type=MESH,
        )

    def send_middle(k, h):
        return pltpu.make_async_remote_copy(
            src_ref=part.at[k, h], dst_ref=other.at[k // 2, h], send_sem=p_ss.at[k, h],
            recv_sem=b_rs.at[k // 2, h], device_id=(inner, c), device_id_type=MESH,
        )

    def share_inner(k, h):
        return pltpu.make_async_remote_copy(
            src_ref=fin.at[k, h], dst_ref=fin.at[k, h], send_sem=fi_ss.at[k, h],
            recv_sem=f_rs.at[k, h], device_id=(inner, c), device_id_type=MESH,
        )

    def share_outer(k, h):
        return pltpu.make_async_remote_copy(
            src_ref=fin.at[k, h], dst_ref=fin.at[k, h], send_sem=fo_ss.at[k, h],
            recv_sem=f_rs.at[k, h], device_id=(outer, c), device_id_type=MESH,
        )

    def save_fin(k, h):
        return pltpu.make_async_copy(
            fin.at[k, h],
            fin_out.at[
                :,
                pl.ds(pl.multiple_of(h * half, half), half),
                pl.ds(pl.multiple_of(k * BLOCK, BLOCK), BLOCK),
            ],
            fin_s.at[k, h],
        )

    def produce(k):
        s = k % SLOTS
        for copy in weights(k):
            copy.wait()

        @pl.when(k + 1 < units)
        def _():
            for copy in weights(k + 1):
                copy.start()

        @pl.loop(0, pieces)
        def _(i):
            at = pl.ds(pl.multiple_of(i * BLOCK, BLOCK), BLOCK)
            keep = keep_in[k, i]
            w_in[s, 0, at, :] = (w_in[s, 0, at, :].astype(F32) * keep).astype(BF16)
            w_in[s, 1, at, :] = (w_in[s, 1, at, :].astype(F32) * keep).astype(BF16)
            w_dn[s, :, at] = (w_dn[s, :, at].astype(F32) * keep_out[k, i]).astype(BF16)

        @pl.loop(0, HALVES)
        def _(h):
            at = pl.ds(pl.multiple_of(h * half, half), half)
            own[k % 2, h, 0] = dot(x[at, :], w_in[s, 0], ((1,), (0,)))
            own[k % 2, h, 1] = dot(x[at, :], w_in[s, 1], ((1,), (0,)))

        @pl.when(k == 0)
        def _():
            gathered(1)

        @pl.loop(0, HALVES)
        def _(h):
            at = pl.ds(pl.multiple_of(h * half, half), half)
            own[k % 2, h, 2] = dot(dy[at, :], w_dn[s], ((1,), (1,)))

    def combine(k):
        b = k % 2

        @pl.loop(0, HALVES)
        def _(h):
            @pl.when(has_outer)
            def _():
                send_inner(k, h).wait_recv()
                for j in range(3):
                    own[b, h, j] += part[k, h, j].astype(F32)

            @pl.when(owns(k))
            def _():
                send_middle(k, h).wait_recv()
                gate = own[b, h, 0] + other[k // 2, h, 0].astype(F32)
                up = own[b, h, 1] + other[k // 2, h, 1].astype(F32)
                grad = own[b, h, 2] + other[k // 2, h, 2].astype(F32)
                sig = jax.nn.sigmoid(gate)
                act = gate * sig
                fin[k, h, 0] = (act * up).astype(BF16)
                fin[k, h, 1] = (grad * up * sig * (1.0 + gate * (1.0 - sig))).astype(BF16)
                fin[k, h, 2] = (grad * act).astype(BF16)
                share_inner(k, h).start()

            @pl.when(jnp.logical_not(owns(k)))
            def _():
                for j in range(3):
                    part[k, h, j] = own[b, h, j].astype(BF16)

                @pl.when(middle)
                def _():
                    send_middle(k, h).start()

                @pl.when(jnp.logical_not(middle))
                def _():
                    send_inner(k, h).start()

            @pl.when(owns(k) & has_outer)
            def _():
                share_outer(k, h).start()

    def consume(k):
        s = k % SLOTS

        @pl.loop(0, HALVES)
        def _(h):
            @pl.when(jnp.logical_not(owns(k)))
            def _():
                share_inner(k, h).wait_recv()

                @pl.when(has_outer)
                def _():
                    share_outer(k, h).start()

            save_fin(k, h).start()

        @pl.loop(0, HALVES)
        def _(h):
            at = pl.ds(pl.multiple_of(h * half, half), half)
            out_acc[at, :] += dot(fin[k, h, 0], w_dn[s], ((1,), (0,)))
            tok_acc[at, :] += dot(fin[k, h, 1], w_in[s, 0], ((1,), (1,))) + dot(
                fin[k, h, 2], w_in[s, 1], ((1,), (1,))
            )

    @pl.loop(0, units + LAG)
    def _(t):
        @pl.when(t < units)
        def _():
            produce(t)

        @pl.when((t >= 1) & (t <= units))
        def _():
            combine(t - 1)

        @pl.when(t >= LAG)
        def _():
            consume(t - LAG)

    def scatters(j):
        return [
            pltpu.make_async_remote_copy(
                src_ref=rs_send.at[
                    j, pl.ds(pl.multiple_of(lax.rem(c + i, cols) * share, share), share), :
                ],
                dst_ref=rs_recv.at[j, i - 1],
                send_sem=rs_ss.at[j, i - 1],
                recv_sem=rs_rs.at[j, i - 1],
                device_id=(r, lax.rem(c + i, cols)),
                device_id_type=MESH,
            )
            for i in range(1, cols)
        ]

    for j, acc in enumerate((out_acc, tok_acc)):
        rs_send[j] = acc[...].astype(BF16)
        for copy in scatters(j):
            copy.start()

    @pl.loop(0, units * HALVES)
    def _(n):
        k, h = n // HALVES, n % HALVES
        save_fin(k, h).wait()

        @pl.when(owns(k))
        def _():
            share_inner(k, h).wait_send()

        @pl.when(jnp.logical_not(owns(k)))
        def _():
            send_inner(k, h).wait_send()

        @pl.when(has_outer)
        def _():
            share_outer(k, h).wait_send()

    for j in range(2):
        saved(j).wait()

    for j, (acc, ref) in enumerate(((out_acc, out), (tok_acc, tok_grad))):
        for copy in scatters(j):
            copy.wait()
        total = acc[mine, :]
        for i in range(cols - 1):
            total = total + rs_recv[j, i].astype(F32)
        ref[...] = total.astype(BF16)


def wgrad_kernel(x, dy, fin, keep_in, keep_out, gate_w, up_w, down_w, x_t, h_t):
    k = pl.program_id(0)
    pieces = x.shape[1] // BLOCK

    @pl.when(k == 0)
    def _():
        @pl.loop(0, pieces)
        def _(i):
            at = pl.ds(pl.multiple_of(i * BLOCK, BLOCK), BLOCK)
            x_t[at, :] = x[:, at].T

    h_t[...] = fin[0].T

    @pl.loop(0, pieces)
    def _(i):
        at = pl.ds(pl.multiple_of(i * BLOCK, BLOCK), BLOCK)

        @pl.when(keep_in[k, i] != 0)
        def _():
            gate_w[at, :] = dot(x_t[at, :], fin[1], ((1,), (0,))).astype(BF16)
            up_w[at, :] = dot(x_t[at, :], fin[2], ((1,), (0,))).astype(BF16)

        @pl.when(keep_in[k, i] == 0)
        def _():
            gate_w[at, :] = jnp.zeros((BLOCK, BLOCK), BF16)
            up_w[at, :] = jnp.zeros((BLOCK, BLOCK), BF16)

        @pl.when(keep_out[k, i] != 0)
        def _():
            down_w[:, at] = dot(h_t[...], dy[:, at], ((1,), (0,))).astype(BF16)

        @pl.when(keep_out[k, i] == 0)
        def _():
            down_w[:, at] = jnp.zeros((BLOCK, BLOCK), BF16)


def local(rows, cols, tokens, w_gate, w_up, w_down, mask_in, mask_out, out_grad):
    share, width = tokens.shape
    hidden = w_gate.shape[1]
    units = hidden // BLOCK
    total = share * cols
    half = total // HALVES
    vmem = pl.BlockSpec(memory_space=pltpu.VMEM)
    smem = pl.BlockSpec(memory_space=pltpu.SMEM)
    anywhere = pl.BlockSpec(memory_space=pl.ANY)
    dma = pltpu.SemaphoreType.DMA
    sent = (units, HALVES)
    flops = 12 * total * width * hidden
    output, tokens_grad, x, dy, fin = pl.pallas_call(
        functools.partial(step_kernel, rows, cols, units),
        out_shape=(
            jax.ShapeDtypeStruct((share, width), BF16),
            jax.ShapeDtypeStruct((share, width), BF16),
            jax.ShapeDtypeStruct((total, width), BF16),
            jax.ShapeDtypeStruct((total, width), BF16),
            jax.ShapeDtypeStruct((3, total, hidden), BF16),
        ),
        in_specs=[vmem, vmem, anywhere, anywhere, anywhere, smem, smem],
        out_specs=(vmem, vmem, anywhere, anywhere, anywhere),
        scratch_shapes=[
            pltpu.VMEM((total, width), BF16),
            pltpu.VMEM((total, width), BF16),
            pltpu.VMEM((units, HALVES, 3, half, BLOCK), BF16),
            pltpu.VMEM(((units + 1) // 2, HALVES, 3, half, BLOCK), BF16),
            pltpu.VMEM((units, HALVES, 3, half, BLOCK), BF16),
            pltpu.VMEM((2, HALVES, 3, half, BLOCK), F32),
            pltpu.VMEM((SLOTS, 2, width, BLOCK), BF16),
            pltpu.VMEM((SLOTS, BLOCK, width), BF16),
            pltpu.VMEM((total, width), F32),
            pltpu.VMEM((total, width), F32),
            pltpu.VMEM((2, total, width), BF16),
            pltpu.VMEM((2, cols - 1, share, width), BF16),
            dma((2, cols - 1)),
            dma((2, cols - 1)),
            dma((2,)),
            dma((SLOTS, 3)),
            dma(sent),
            dma(sent),
            dma(((units + 1) // 2, HALVES)),
            dma(sent),
            dma(sent),
            dma(sent),
            dma((2,)),
            dma(sent),
            dma((2, cols - 1)),
            dma((2, cols - 1)),
        ],
        compiler_params=pltpu.CompilerParams(
            collective_id=0, has_side_effects=True, vmem_limit_bytes=63 * 1024 * 1024
        ),
        cost_estimate=pl.CostEstimate(
            flops=flops, bytes_accessed=6 * width * hidden, transcendentals=total * hidden
        ),
        name="step",
    )(
        tokens, out_grad, w_gate, w_up, w_down,
        mask_in.astype(F32), mask_out.astype(F32),
    )
    gate_wgrad, up_wgrad, down_wgrad = pl.pallas_call(
        wgrad_kernel,
        grid=(units,),
        out_shape=(
            jax.ShapeDtypeStruct((width, hidden), BF16),
            jax.ShapeDtypeStruct((width, hidden), BF16),
            jax.ShapeDtypeStruct((hidden, width), BF16),
        ),
        in_specs=[
            pl.BlockSpec((total, width), lambda k: (0, 0)),
            pl.BlockSpec((total, width), lambda k: (0, 0)),
            pl.BlockSpec((3, total, BLOCK), lambda k: (0, 0, k)),
            smem,
            smem,
        ],
        out_specs=(
            pl.BlockSpec((width, BLOCK), lambda k: (0, k)),
            pl.BlockSpec((width, BLOCK), lambda k: (0, k)),
            pl.BlockSpec((BLOCK, width), lambda k: (k, 0)),
        ),
        scratch_shapes=[pltpu.VMEM((width, total), BF16), pltpu.VMEM((BLOCK, total), BF16)],
        compiler_params=pltpu.CompilerParams(vmem_limit_bytes=40 * 1024 * 1024),
        name="wgrad",
    )(x, dy, fin, mask_in, mask_out)
    return output, tokens_grad, gate_wgrad, up_wgrad, down_wgrad


def solution(mesh):
    placed = (
        P("col", "row"),
        P("row", "col"),
        P("row", "col"),
        P("col", "row"),
        P("col", "row"),
        P("col", "row"),
        P("col", "row"),
    )
    return jax.shard_map(
        functools.partial(local, mesh.shape["row"], mesh.shape["col"]),
        mesh=mesh,
        in_specs=placed,
        out_specs=(
            P("col", "row"),
            P("col", "row"),
            P("row", "col"),
            P("row", "col"),
            P("col", "row"),
        ),
        check_vma=False,
    )
```
